256 devices in a mesh: row: 16 (over y, x), col: 16 (over z, core).
Axes of the slice: x: 4, y: 4, z: 8, core: 2. Of those that a mesh axis runs over, the one named last changes fastest.
Arguments:
- matrix: float32 [8, 16, 128, 8, 16, 128], P(None, 'row', None, None, 'col'), as said below
Outputs:
- updated: float32 [8, 16, 128, 8, 16, 128], P(None, 'row', None, None, 'col')
- images: float32 [8, 8, 16, 128], P(None, None, 'row')
Inputs may be any that keep to these rules, and one draw needn't show every extreme that they name: The matrix is symmetric: entry (r, c) equals entry (c, r).
All inputs are finite; a program needn't handle non-finite values.
Results may differ from the reference program's by a relative error of at most 0.00016.
Values sent between devices are 32-bit elements; how exact they have to be, the bound alone decides.
No kernel may reach another device: no remote copies, remote signals or barrier semaphores. Data moves between devices by JAX's collectives and lax.ppermute only.
A program may use at most 128 MiB of HBM per device.

```python
import math
import jax
import jax.numpy as jnp
from jax import lax

N = 16384
NB = 128
K = 8
LR = 8
LC = 8
N_ROW = 16
N_COL = 16


def draw_matrix(key, part):
    first_key = jax.random.fold_in(key, 11)
    row_ids = jnp.arange(N, dtype=jnp.int32)
    block_pos = (row_ids // NB % N_ROW).astype(jnp.float32) / (N_ROW - 1)
    base_scale = jnp.exp((block_pos - 0.5) * math.log(3.0))
    entries = jax.random.truncated_normal(first_key, -6.0, 6.0, (N, N), jnp.float32)
    row_scale = base_scale
    symmetric = (entries + entries.T) * 0.70710678
    scaled = row_scale[:, None] * symmetric * row_scale[None, :]
    return scaled.reshape(LR, N_ROW, NB, LC, N_COL, NB)


def setup_inputs(seed: int = 0) -> dict:
    key_of = jax.random.split(jax.random.key(seed), 2)
    return {
        "matrix": draw_matrix(jax.random.fold_in(key_of[1], 71), 0),
    }


epsilon = 1e-06
highest = lax.Precision.HIGHEST

def product(left_side, right_side):
    return jnp.dot(left_side, right_side, precision=highest)

def reference(matrix):
    square = matrix.reshape(N, N)
    row_ids = jnp.arange(N, dtype=jnp.int32)
    reflectors = jnp.zeros((N, K), jnp.float32)
    images_mat = jnp.zeros((N, K), jnp.float32)
    for position in range(K):
        column = square[:, position] - product(reflectors, images_mat[position]) - product(images_mat, reflectors[position])
        below_diag = jnp.where(row_ids > position, column, jnp.zeros_like(column))
        col_norm = jnp.sqrt(jnp.sum(below_diag * below_diag))
        first_entry = column[position + 1]
        vector = below_diag + jnp.where(row_ids == position + 1, col_norm, jnp.zeros_like(column))
        reflector = vector / jnp.sqrt(2.0 * col_norm * (col_norm + first_entry) + epsilon)
        image_vec = product(square, reflector) - product(reflectors, product(images_mat.T, reflector)) - product(images_mat, product(reflectors.T, reflector))
        gamma_val = product(reflector, image_vec)
        update = 2.0 * image_vec - 2.0 * gamma_val * reflector
        reflectors = reflectors.at[:, position].set(reflector)
        images_mat = images_mat.at[:, position].set(update)
    left_side = jnp.concatenate([reflectors, images_mat], axis=1)
    right_side = jnp.concatenate([images_mat, reflectors], axis=1)
    updated = square - product(left_side, right_side.T)
    return (updated.reshape(matrix.shape), images_mat.T.reshape(K, LR, N_ROW, NB))
```

```python
import functools

import jax
import jax.numpy as jnp
from jax import lax
from jax.experimental import pallas as pl
from jax.experimental.pallas import tpu as pltpu
from jax.sharding import PartitionSpec as P

K = 8
EPS = 1e-06
PEERS = 16
F32 = jnp.float32
SCOPED = 16 * 1024 * 1024


def vmem():
    return pl.BlockSpec(memory_space=pltpu.VMEM)


def smem():
    return pl.BlockSpec(memory_space=pltpu.SMEM)


def head(slab, entry):
    return jnp.broadcast_to(slab[0:1, entry : entry + 1], slab.shape)


def total(slab):
    by_lane = jnp.sum(slab, axis=0, keepdims=True)
    return jnp.broadcast_to(jnp.sum(by_lane, axis=1, keepdims=True), slab.shape)


def dot(left, right):
    return total(jnp.sum(left * right, axis=0))


def slab_index(shape, axis):
    return lax.broadcasted_iota(jnp.int32, shape, axis)


def full_ids():
    shape = (PEERS, 8, 128)
    first = (slab_index(shape, 0) == 0) & (slab_index(shape, 1) == 0)
    return jnp.where(first, slab_index(shape, 2), 1024)


def own_ids(mine):
    shape = (8, 128)
    first = (slab_index(shape, 0) == 0) & (mine == 0)
    return jnp.where(first, slab_index(shape, 1), 1024)


def times_cols(tile, x, out):
    def rows(a, carry):
        start = pl.multiple_of(a * 128, 128)
        acc = tile[0, pl.ds(start, 128), :] * x[0:1, :]
        for b in range(1, 8):
            acc += tile[b, pl.ds(start, 128), :] * x[b : b + 1, :]
        out[pl.ds(a, 1), :] = jnp.sum(acc.T, axis=0, keepdims=True)
        return carry

    lax.fori_loop(0, 8, rows, 0)


def times_rows(tile, x_ref, out):
    def rows(a, sums):
        start = pl.multiple_of(a * 128, 128)
        x = jnp.broadcast_to(x_ref[pl.ds(a, 1), :], (128, 128)).T
        return tuple(
            s + jnp.sum((tile[b, pl.ds(start, 128), :] * x).reshape(16, 8, 128), axis=0)
            for b, s in enumerate(sums)
        )

    sums = lax.fori_loop(0, 8, rows, (jnp.zeros((8, 128), F32),) * 8)
    for b in range(8):
        out[b : b + 1, :] = jnp.sum(sums[b], axis=0, keepdims=True)


def send(payload, slabs):
    for n, slab in enumerate(slabs):
        for q in range(PEERS):
            payload[q, n] = slab


def first_kernel(place, panel, tile, payload, product):
    x = jnp.where(own_ids(place[1]) > 0, panel[0], 0.0)
    times_cols(tile, x, product)
    send(payload, [product[...], panel[0], panel[1]])


def finish_image(j, got, us, ws, coeffs):
    y = got
    for k in range(j):
        y = y - us[k][...] * coeffs[k] - ws[k][...] * coeffs[K + k]
    gamma = dot(us[j][...], y)
    return y, gamma, 2.0 * y - 2.0 * gamma * us[j][...]


def step_kernel(j, *refs):
    refs = list(refs)
    place, got, panel = refs[:3]
    del refs[:3]
    late = refs.pop(0) if j % 2 else got
    tile = refs.pop(0) if j < K - 1 else None
    us = [refs.pop(0) for _ in range(j)]
    ws = [refs.pop(0) for _ in range(max(j - 1, 0))]
    coeffs_before = refs.pop(0) if j > 0 else None
    payload, u_out, coeffs = refs[:3]
    del refs[:3]
    if j > 0:
        w_out = refs.pop(0)
    y_ref, x_ref, product = refs
    mine = place[j % 2]
    ids = full_ids()
    summed = got[0, 0]
    for q in range(1, PEERS):
        summed = summed + got[q, 0]
    at = {0: 1, 1: 2}.get(j, 3 if j % 2 else 2)
    column, column_own = late[:, at], late[mine, at]
    next_own = panel[j + 1] if j % 2 else late[mine, at + 1]
    x = column
    if j > 0:
        y, gamma, w = finish_image(j - 1, got[:, 1], us, ws, coeffs_before)
        w_out[...] = w
        ws = ws + [w_out]
        bend = head(us[j - 1][0], j)
        alpha = 4.0 * gamma * bend - 2.0 * head(y[0], j)
        summed = summed + alpha * (got[mine, 1] - bend * column_own)
        for k in range(j):
            x = x - us[k][...] * head(ws[k][0], j) - ws[k][...] * head(us[k][0], j)
    x = jnp.where(ids > j, x, 0.0)
    norm = jnp.sqrt(dot(x, x))
    denom = jnp.sqrt(2.0 * norm * (norm + head(x[0], j + 1)) + EPS)
    u = (x + jnp.where(ids == j + 1, norm, 0.0)) / denom
    u_out[...] = u
    image = (summed + norm * next_own) / denom
    for k in range(j):
        coeffs[k] = dot(ws[k][...], u)
        coeffs[K + k] = dot(us[k][...], u)
    if j == K - 1:
        send(payload, [image])
        return
    y_own = image
    x_own = next_own
    for k in range(j):
        u_own, w_own = us[k][mine], ws[k][mine]
        y_own = y_own - u_own * coeffs[k] - w_own * coeffs[K + k]
        x_own = x_own - u_own * head(ws[k][0], j + 1) - w_own * head(us[k][0], j + 1)
    x_own = x_own - 2.0 * head(u[0], j + 1) * y_own
    x_own = jnp.where(own_ids(mine) > j + 1, x_own, 0.0)
    x_ref[...] = x_own
    if j % 2:
        times_cols(tile, x_own, product)
        send(payload, [product[...], image, panel[j + 1], panel[j + 2]])
    else:
        times_rows(tile, x_ref, product)
        send(payload, [product[...], image])


ROWS = 128


def last_kernel(place, got, coeffs, *refs):
    us, ws = refs[:K], list(refs[K : 2 * K - 1])
    block, updated, images, w_ref, right, left = refs[2 * K - 1 :]
    row, col = place[0], place[1]

    @pl.when(pl.program_id(0) == 0)
    def _():
        _, _, w = finish_image(K - 1, got[:, 0], us, ws, coeffs)
        w_ref[...] = w
        all_ws = ws + [w_ref]
        for k in range(K):
            images[k] = all_ws[k][row]
            right[pl.ds(8 * k, 8), :] = all_ws[k][col]
            right[pl.ds(8 * (K + k), 8), :] = us[k][col]
        for a in range(8):
            lines = [v[row, a : a + 1] for v in [*us, *all_ws]]
            wide = jnp.concatenate([jnp.broadcast_to(v, (8, 128)) for v in lines], axis=0)
            left[a] = wide.T

    mask = jnp.where(
        slab_index((8, 128), 1) % 8 == slab_index((8, 128), 0), 1.0, 0.0
    )
    wide = left[pl.program_id(0)]
    spread = (wide[:, None, :] * mask[None, :, :]).reshape(ROWS * 8, 128)
    change = jnp.dot(spread, right[...], precision=lax.Precision.HIGHEST, preferred_element_type=F32)
    updated[...] = block[...] - change.reshape(ROWS, 8, 128)


def params():
    return pltpu.CompilerParams(vmem_limit_bytes=SCOPED)


def cost(flops, moved):
    return pl.CostEstimate(flops=flops, bytes_accessed=moved, transcendentals=0)


def exchange(payload, axis):
    return lax.all_to_all(payload, axis, split_axis=0, concat_axis=0, tiled=True)


def body(matrix):
    whole = jax.ShapeDtypeStruct((PEERS, 8, 128), F32)
    native = matrix.reshape(1024, 8, 128)
    place = jnp.stack([lax.axis_index("row"), lax.axis_index("col")]).astype(jnp.int32)
    panel = exchange(jnp.broadcast_to(native[None, : K + 1], (PEERS, K + 1, 8, 128)), "row")[0]
    tile = native.transpose(1, 0, 2)
    payload = pl.pallas_call(
        first_kernel,
        out_shape=jax.ShapeDtypeStruct((PEERS, 3, 8, 128), F32),
        in_specs=[smem(), vmem(), vmem()],
        out_specs=vmem(),
        scratch_shapes=[pltpu.VMEM((8, 128), F32)],
        compiler_params=params(),
        cost_estimate=cost(2**21, 2**22),
    )(place, panel, tile)
    us, ws, coeffs, before = [], [], None, None
    for j in range(K):
        got = exchange(payload, "row" if j % 2 else "col")
        inputs = [place, got, panel]
        if j % 2:
            inputs.append(before)
        if j < K - 1:
            inputs.append(tile)
        inputs += us + ws
        if j > 0:
            inputs.append(coeffs)
        sent = 1 if j == K - 1 else (4 if j % 2 else 2)
        outs = [jax.ShapeDtypeStruct((PEERS, sent, 8, 128), F32), whole, whole]
        if j > 0:
            outs.append(whole)
        results = pl.pallas_call(
            functools.partial(step_kernel, j),
            out_shape=outs,
            in_specs=[smem()] + [vmem()] * (len(inputs) - 1),
            out_specs=[vmem()] * len(outs),
            scratch_shapes=[pltpu.VMEM((8, 128), F32)] * 3,
            compiler_params=params(),
            cost_estimate=cost(2**21, 2**22),
            name=f"step_{j}",
        )(*inputs)
        payload, coeffs = results[0], results[2]
        us.append(results[1])
        if j > 0:
            ws.append(results[3])
        before = got
    got = exchange(payload, "col")
    fixed = lambda s: pl.BlockSpec(s, lambda i: (0,) * len(s))
    slab = fixed((PEERS, 8, 128))
    updated, images = pl.pallas_call(
        last_kernel,
        grid=(1024 // ROWS,),
        out_shape=(jax.ShapeDtypeStruct((1024, 8, 128), F32), jax.ShapeDtypeStruct((K, 8, 128), F32)),
        in_specs=[smem(), fixed((PEERS, 1, 8, 128)), slab]
        + [slab] * (2 * K - 1)
        + [pl.BlockSpec((ROWS, 8, 128), lambda i: (i, 0, 0))],
        out_specs=[pl.BlockSpec((ROWS, 8, 128), lambda i: (i, 0, 0)), fixed((K, 8, 128))],
        scratch_shapes=[
            pltpu.VMEM((PEERS, 8, 128), F32),
            pltpu.VMEM((128, 128), F32),
            pltpu.VMEM((8, 128, 128), F32),
        ],
        compiler_params=params(),
        cost_estimate=cost(2**25, 2**23),
    )(place, got, coeffs, *us, *ws, native)
    return updated.reshape(matrix.shape), images.reshape(K, 8, 1, 128)


def solution(mesh):
    spec = P(None, "row", None, None, "col", None)
    return jax.shard_map(
        body, mesh=mesh, in_specs=(spec,), out_specs=(spec, P(None, None, "row", None)), check_vma=False
    )
```

```python
import functools

import jax
import jax.numpy as jnp
from jax import lax
from jax.experimental import pallas as pl
from jax.experimental.pallas import tpu as pltpu
from jax.sharding import PartitionSpec as P

K = 8
EPS = 1e-06
PEERS = 16
F32 = jnp.float32
SCOPED = 16 * 1024 * 1024
WIDE = 62000000


def vmem():
    return pl.BlockSpec(memory_space=pltpu.VMEM)


def smem():
    return pl.BlockSpec(memory_space=pltpu.SMEM)


def head(slab, entry):
    return jnp.broadcast_to(slab[0:1, entry : entry + 1], slab.shape)


def total(slab):
    by_lane = jnp.sum(slab, axis=0, keepdims=True)
    return jnp.broadcast_to(jnp.sum(by_lane, axis=1, keepdims=True), slab.shape)


def dot(left, right):
    return total(jnp.sum(left * right, axis=0))


def slab_index(shape, axis):
    return lax.broadcasted_iota(jnp.int32, shape, axis)


def full_ids():
    shape = (PEERS, 8, 128)
    first = (slab_index(shape, 0) == 0) & (slab_index(shape, 1) == 0)
    return jnp.where(first, slab_index(shape, 2), 1024)


def own_ids(mine):
    shape = (8, 128)
    first = (slab_index(shape, 0) == 0) & (mine == 0)
    return jnp.where(first, slab_index(shape, 1), 1024)


def times_cols(tile, x, out):
    def rows(a, carry):
        start = pl.multiple_of(a * 128, 128)
        acc = tile[0, pl.ds(start, 128), :] * x[0:1, :]
        for b in range(1, 8):
            acc += tile[b, pl.ds(start, 128), :] * x[b : b + 1, :]
        out[pl.ds(a, 1), :] = jnp.sum(acc.T, axis=0, keepdims=True)
        return carry

    lax.fori_loop(0, 8, rows, 0)


def times_rows(tile, x_ref, out):
    def rows(a, sums):
        start = pl.multiple_of(a * 128, 128)
        x = jnp.broadcast_to(x_ref[pl.ds(a, 1), :], (128, 128)).T
        return tuple(
            s + jnp.sum((tile[b, pl.ds(start, 128), :] * x).reshape(16, 8, 128), axis=0)
            for b, s in enumerate(sums)
        )

    sums = lax.fori_loop(0, 8, rows, (jnp.zeros((8, 128), F32),) * 8)
    for b in range(8):
        out[b : b + 1, :] = jnp.sum(sums[b], axis=0, keepdims=True)


def send(payload, slabs):
    for n, slab in enumerate(slabs):
        for q in range(PEERS):
            payload[q, n] = slab


def panel_kernel(matrix, payload, corner, panel, sem):
    copies = []
    for a in range(8):
        rows = pl.ds(128 * a, 128)
        copies.append(pltpu.make_async_copy(matrix.at[rows, 0, :], corner.at[rows], sem.at[a]))
        copies[-1].start()
    for a in range(8):
        copies[a].wait()
        lines = corner[pl.ds(128 * a, 128), :].T
        for k in range(K + 1):
            panel[k, a : a + 1, :] = lines[k : k + 1, :]
    for q in range(PEERS):
        payload[q, 0] = panel[0]
        payload[q, 1] = panel[1]
        payload[q, 2] = panel[2 + q % (K - 1)]


def load_kernel(matrix, tile, spare, held, fetched, stored):
    into = [pltpu.make_async_copy(matrix.at[:, b, :], held.at[b], fetched.at[b]) for b in range(8)]
    out = [
        pltpu.make_async_copy(held.at[b], ref.at[b], stored.at[n, b])
        for b in range(8)
        for n, ref in enumerate((tile, spare))
    ]
    for copy in into:
        copy.start()
    for b in range(8):
        into[b].wait()
        out[2 * b].start()
        out[2 * b + 1].start()
    for copy in out:
        copy.wait()


def first_kernel(place, panel, tile, payload, held, x_ref, lines, sem):
    copies = [pltpu.make_async_copy(tile.at[b], held.at[b], sem.at[b]) for b in range(8)]
    for copy in copies:
        copy.start()
    x_ref[...] = jnp.where(own_ids(place[0]) > 0, panel[0, 0], 0.0)
    for a in range(8):
        lines[pl.ds(128 * a, 128), :] = jnp.broadcast_to(x_ref[a : a + 1, :], (128, 128)).T
    for b in range(8):
        copies[b].wait()

        def rows(a, acc):
            at = pl.ds(pl.multiple_of(a * 128, 128), 128)
            return acc + jnp.sum((held[b, at, :] * lines[at, :]).reshape(16, 8, 128), axis=0)

        line = jnp.sum(lax.fori_loop(0, 8, rows, jnp.zeros((8, 128), F32)), axis=0, keepdims=True)
        for q in range(PEERS):
            payload[q, 0, b : b + 1, :] = line
    for q in range(PEERS):
        payload[q, 1] = panel[0, 0]
        payload[q, 2] = panel[0, 1]


def finish_image(j, got, us, ws, coeffs):
    y = got
    for k in range(j):
        y = y - us[k][...] * coeffs[k] - ws[k][...] * coeffs[K + k]
    gamma = dot(us[j][...], y)
    return y, gamma, 2.0 * y - 2.0 * gamma * us[j][...]


def step_kernel(j, *refs):
    refs = list(refs)
    place, got = refs[:2]
    del refs[:2]
    spare = got if j == 1 else refs.pop(0) if j == 0 or j % 2 else None
    late = refs.pop(0) if j % 2 else got
    tile = refs.pop(0) if j < K - 1 else None
    us = [refs.pop(0) for _ in range(j)]
    ws = [refs.pop(0) for _ in range(max(j - 1, 0))]
    coeffs_before = refs.pop(0) if j > 0 else None
    payload, u_out, coeffs = refs[:3]
    del refs[:3]
    if j > 0:
        w_out = refs.pop(0)
    x_ref, product = refs
    mine = place[(j + 1) % 2]
    ids = full_ids()
    summed = got[0, 0]
    for q in range(1, PEERS):
        summed = summed + got[q, 0]
    at = {0: 1, 1: 2}.get(j, 3 if j % 2 else 2)
    column, column_own = late[:, at], late[mine, at]
    next_own = spare[j - 1, 2] if j % 2 else late[mine, at + 1]
    x = column
    if j > 0:
        y, gamma, w = finish_image(j - 1, got[:, 1], us, ws, coeffs_before)
        w_out[...] = w
        ws = ws + [w_out]
        bend = head(us[j - 1][0], j)
        alpha = 4.0 * gamma * bend - 2.0 * head(y[0], j)
        summed = summed + alpha * (got[mine, 1] - bend * column_own)
        for k in range(j):
            x = x - us[k][...] * head(ws[k][0], j) - ws[k][...] * head(us[k][0], j)
    x = jnp.where(ids > j, x, 0.0)
    norm = jnp.sqrt(dot(x, x))
    denom = jnp.sqrt(2.0 * norm * (norm + head(x[0], j + 1)) + EPS)
    u = (x + jnp.where(ids == j + 1, norm, 0.0)) / denom
    u_out[...] = u
    image = (summed + norm * next_own) / denom
    for k in range(j):
        coeffs[k] = dot(ws[k][...], u)
        coeffs[K + k] = dot(us[k][...], u)
    if j == K - 1:
        send(payload, [image])
        return
    y_own = image
    x_own = next_own
    for k in range(j):
        u_own, w_own = us[k][mine], ws[k][mine]
        y_own = y_own - u_own * coeffs[k] - w_own * coeffs[K + k]
        x_own = x_own - u_own * head(ws[k][0], j + 1) - w_own * head(us[k][0], j + 1)
    x_own = x_own - 2.0 * head(u[0], j + 1) * y_own
    x_own = jnp.where(own_ids(mine) > j + 1, x_own, 0.0)
    x_ref[...] = x_own
    if j % 2:
        times_rows(tile, x_ref, product)
        send(payload, [product[...], image, spare[j - 1, 2], spare[j, 2]])
    else:
        times_cols(tile, x_own, product)
        send(payload, [product[...], image] + ([spare[0, 2]] if j == 0 else []))


def thirds(value):
    high = value.astype(jnp.bfloat16).astype(F32)
    rest = value - high
    middle = rest.astype(jnp.bfloat16).astype(F32)
    return high, middle, rest - middle


def last_kernel(place, got, coeffs, *refs):
    us, ws = refs[:K], list(refs[K : 2 * K - 1])
    tile, updated, images, w_ref, right, result, sem = refs[2 * K - 1 :]
    row, col = place[0], place[1]
    _, _, w = finish_image(K - 1, got[:, 0], us, ws, coeffs)
    w_ref[...] = w
    ws = ws + [w_ref]
    for k in range(K):
        images[k] = ws[k][row]
    pad = jnp.zeros((32, 128), F32)
    for b in range(8):
        high, middle, low = thirds(jnp.concatenate([v[col, b : b + 1] for v in [*ws, *us]], axis=0))
        right[:, 128 * b : 128 * (b + 1)] = jnp.concatenate(
            [high, middle, high, low, middle, high, pad], axis=0
        ).astype(jnp.bfloat16)
    copies = []
    for a in range(8):
        high, middle, low = thirds(jnp.concatenate([v[row, a : a + 1] for v in [*us, *ws]], axis=0))
        left = jnp.concatenate([high, high, middle, high, middle, low, pad], axis=0).T.astype(jnp.bfloat16)
        change = jnp.dot(left, right[...], preferred_element_type=F32)
        for b in range(8):
            rows = pl.ds(128 * a, 128)
            result[b, rows, :] = tile[b, rows, :] - change[:, 128 * b : 128 * (b + 1)]
            copies.append(
                pltpu.make_async_copy(result.at[b, rows, :], updated.at[rows, b, :], sem.at[8 * a + b])
            )
            copies[-1].start()
    for copy in copies:
        copy.wait()


def params(limit=SCOPED):
    return pltpu.CompilerParams(vmem_limit_bytes=limit)


def cost(flops, moved):
    return pl.CostEstimate(flops=flops, bytes_accessed=moved, transcendentals=0)


def exchange(payload, axis):
    return lax.all_to_all(payload, axis, split_axis=0, concat_axis=0, tiled=True)


def body(matrix):
    whole = jax.ShapeDtypeStruct((PEERS, 8, 128), F32)
    native = matrix.reshape(1024, 8, 128)
    place = jnp.stack([lax.axis_index("row"), lax.axis_index("col")]).astype(jnp.int32)
    hbm = pl.BlockSpec(memory_space=pltpu.HBM)
    payload = pl.pallas_call(
        panel_kernel,
        out_shape=jax.ShapeDtypeStruct((PEERS, 3, 8, 128), F32),
        in_specs=[hbm],
        out_specs=vmem(),
        scratch_shapes=[
            pltpu.VMEM((1024, 128), F32),
            pltpu.VMEM((K + 1, 8, 128), F32),
            pltpu.SemaphoreType.DMA((8,)),
        ],
        compiler_params=params(WIDE),
        cost_estimate=cost(2**20, 2**20),
    )(native)
    panel = exchange(payload, "col")
    streamed, plain = pl.pallas_call(
        load_kernel,
        out_shape=(
            jax.ShapeDtypeStruct((40, 1024, 128), F32),
            jax.ShapeDtypeStruct((8, 1024, 128), F32),
        ),
        in_specs=[hbm],
        out_specs=[hbm, hbm],
        scratch_shapes=[
            pltpu.VMEM((8, 1024, 128), F32),
            pltpu.SemaphoreType.DMA((8,)),
            pltpu.SemaphoreType.DMA((2, 8)),
        ],
        compiler_params=params(WIDE),
        cost_estimate=cost(2**21, 2**23),
    )(native)
    payload, tile = pl.pallas_call(
        first_kernel,
        out_shape=(
            jax.ShapeDtypeStruct((PEERS, 3, 8, 128), F32),
            jax.ShapeDtypeStruct((8, 1024, 128), F32),
        ),
        in_specs=[smem(), vmem(), hbm],
        out_specs=[vmem(), vmem()],
        scratch_shapes=[
            pltpu.VMEM((8, 128), F32),
            pltpu.VMEM((1024, 128), F32),
            pltpu.SemaphoreType.DMA((8,)),
        ],
        compiler_params=params(48000000),
        cost_estimate=cost(2**21, 2**22),
    )(place, panel, streamed)
    us, ws, coeffs, before = [], [], None, None
    for j in range(K):
        got = exchange(payload, "col" if j % 2 else "row")
        inputs = [place, got]
        if j == 0:
            inputs.append(panel)
        if j == 1:
            spare = got
        elif j % 2:
            inputs.append(spare)
        if j % 2:
            inputs.append(before)
        if j < K - 1:
            inputs.append(tile)
        inputs += us + ws
        if j > 0:
            inputs.append(coeffs)
        sent = 1 if j == K - 1 else 3 if j == 0 else 4 if j % 2 else 2
        outs = [jax.ShapeDtypeStruct((PEERS, sent, 8, 128), F32), whole, whole]
        if j > 0:
            outs.append(whole)
        results = pl.pallas_call(
            functools.partial(step_kernel, j),
            out_shape=outs,
            in_specs=[smem()] + [vmem()] * (len(inputs) - 1),
            out_specs=[vmem()] * len(outs),
            scratch_shapes=[pltpu.VMEM((8, 128), F32)] * 2,
            compiler_params=params(),
            cost_estimate=cost(2**21, 2**22),
            name=f"step_{j}",
        )(*inputs)
        payload, coeffs = results[0], results[2]
        us.append(results[1])
        if j > 0:
            ws.append(results[3])
        before = got
    got = exchange(payload, "row")
    updated, images = pl.pallas_call(
        last_kernel,
        out_shape=(jax.ShapeDtypeStruct((1024, 8, 128), F32), jax.ShapeDtypeStruct((K, 8, 128), F32)),
        in_specs=[smem()] + [vmem()] * (2 * K + 2),
        out_specs=[hbm, vmem()],
        scratch_shapes=[
            pltpu.VMEM((PEERS, 8, 128), F32),
            pltpu.VMEM((128, 1024), jnp.bfloat16),
            pltpu.VMEM((8, 1024, 128), F32),
            pltpu.SemaphoreType.DMA((64,)),
        ],
        compiler_params=params(),
        cost_estimate=cost(2**25, 2**23),
    )(place, got, coeffs, *us, *ws, plain)
    return updated.reshape(matrix.shape), images.reshape(K, 8, 1, 128)


def solution(mesh):
    spec = P(None, "row", None, None, "col", None)
    return jax.shard_map(
        body, mesh=mesh, in_specs=(spec,), out_specs=(spec, P(None, None, "row", None)), check_vma=False
    )
```

```python
import functools

import jax
import jax.numpy as jnp
from jax import lax
from jax.experimental import pallas as pl
from jax.experimental.pallas import tpu as pltpu
from jax.sharding import PartitionSpec as P

K = 8
EPS = 1e-06
PEERS = 16
F32 = jnp.float32
SCOPED = 16 * 1024 * 1024
WIDE = 62000000


def vmem():
    return pl.BlockSpec(memory_space=pltpu.VMEM)


def smem():
    return pl.BlockSpec(memory_space=pltpu.SMEM)


def head(slab, entry):
    return jnp.broadcast_to(slab[0:1, entry : entry + 1], slab.shape)


def total(slab):
    by_lane = jnp.sum(slab, axis=0, keepdims=True)
    return jnp.broadcast_to(jnp.sum(by_lane, axis=1, keepdims=True), slab.shape)


def dot(left, right):
    return total(jnp.sum(left * right, axis=0))


def slab_index(shape, axis):
    return lax.broadcasted_iota(jnp.int32, shape, axis)


def full_ids():
    shape = (PEERS, 8, 128)
    first = (slab_index(shape, 0) == 0) & (slab_index(shape, 1) == 0)
    return jnp.where(first, slab_index(shape, 2), 1024)


def own_ids(mine):
    shape = (8, 128)
    first = (slab_index(shape, 0) == 0) & (mine == 0)
    return jnp.where(first, slab_index(shape, 1), 1024)


def times_cols(tile, x, out):
    for a in range(8):
        rows = pl.ds(a * 128, 128)
        acc = tile[0, rows, :] * x[0:1, :]
        for b in range(1, 8):
            acc += tile[b, rows, :] * x[b : b + 1, :]
        out[a : a + 1, :] = jnp.sum(acc.T, axis=0, keepdims=True)


def times_rows(tile, x_ref, out):
    sums = [jnp.zeros((8, 128), F32)] * 8
    for a in range(8):
        x = jnp.broadcast_to(x_ref[a : a + 1, :], (128, 128)).T
        for b in range(8):
            line = tile[b, pl.ds(a * 128, 128), :] * x
            sums[b] += jnp.sum(line.reshape(16, 8, 128), axis=0)
    for b in range(8):
        out[b : b + 1, :] = jnp.sum(sums[b], axis=0, keepdims=True)


def send(payload, slabs):
    for n, slab in enumerate(slabs):
        for q in range(PEERS):
            payload[q, n] = slab


def panel_kernel(matrix, payload, corner, panel, sem):
    copies = []
    for a in range(8):
        rows = pl.ds(128 * a, 128)
        copies.append(pltpu.make_async_copy(matrix.at[rows, 0, :], corner.at[rows], sem.at[a]))
        copies[-1].start()
    for a in range(8):
        copies[a].wait()
        lines = corner[pl.ds(128 * a, 128), :].T
        for k in range(K + 1):
            panel[k, a : a + 1, :] = lines[k : k + 1, :]
    for q in range(PEERS):
        payload[q, 0] = panel[0]
        payload[q, 1] = panel[1]
        payload[q, 2] = panel[2 + q % (K - 1)]


def load_kernel(matrix, tile, spare, held, fetched, stored):
    into = [pltpu.make_async_copy(matrix.at[:, b, :], held.at[b], fetched.at[b]) for b in range(8)]
    out = [
        pltpu.make_async_copy(held.at[b], ref.at[b], stored.at[n, b])
        for b in range(8)
        for n, ref in enumerate((tile, spare))
    ]
    for copy in into:
        copy.start()
    for b in range(8):
        into[b].wait()
        out[2 * b].start()
        out[2 * b + 1].start()
    for copy in out:
        copy.wait()


def first_kernel(place, panel, tile, payload, held, x_ref, lines, sem):
    copies = [pltpu.make_async_copy(tile.at[b], held.at[b], sem.at[b]) for b in range(8)]
    for copy in copies:
        copy.start()
    x_ref[...] = jnp.where(own_ids(place[0]) > 0, panel[0, 0], 0.0)
    for a in range(8):
        lines[pl.ds(128 * a, 128), :] = jnp.broadcast_to(x_ref[a : a + 1, :], (128, 128)).T
    for b in range(8):
        copies[b].wait()
        line = jnp.sum((held[b] * lines[...]).reshape(128, 8, 128), axis=0)
        line = jnp.sum(line, axis=0, keepdims=True)
        for q in range(PEERS):
            payload[q, 0, b : b + 1, :] = line
    for q in range(PEERS):
        payload[q, 1] = panel[0, 0]
        payload[q, 2] = panel[0, 1]


def rayleigh(j, product, u, coeffs):
    gamma = dot(u, product)
    for k in range(j):
        gamma = gamma - 2.0 * coeffs[k] * coeffs[K + k]
    return gamma


def image(j, product, us, ws, coeffs, gamma):
    y = product
    for k in range(j):
        y = y - us[k] * coeffs[k] - ws[k] * coeffs[K + k]
    return y, 2.0 * y - 2.0 * gamma * us[j]


def step_kernel(j, *refs):
    refs = list(refs)
    place, got = refs[:2]
    del refs[:2]
    spare = got if j == 1 else refs.pop(0) if j == 0 or j % 2 else None
    late = refs.pop(0) if j % 2 else got
    tile = refs.pop(0) if j < K - 1 else None
    us = [refs.pop(0) for _ in range(j)]
    ws = [refs.pop(0) for _ in range(max(j - 1, 0))]
    coeffs_before = refs.pop(0) if j > 0 else None
    payload, u_out, coeffs = refs[:3]
    del refs[:3]
    if j > 0:
        w_out = refs.pop(0)
    x_ref, product = refs
    mine = place[(j + 1) % 2]
    ids = full_ids()
    summed = got[0, 0]
    for q in range(1, PEERS):
        summed = summed + got[q, 0]
    at = {0: 1, 1: 2}.get(j, 3 if j % 2 else 2)
    column, column_own = late[:, at], late[mine, at]
    next_own = spare[j - 1, 2] if j % 2 else late[mine, at + 1]
    x = column
    if j > 0:
        before = got[:, 1]
        gamma = rayleigh(j - 1, before, us[j - 1][...], coeffs_before)
        y, w = image(
            j - 1, before, [v[...] for v in us], [v[...] for v in ws], coeffs_before, gamma
        )
        w_out[...] = w
        ws = ws + [w_out]
        bend = head(us[j - 1][0], j)
        alpha = 4.0 * gamma * bend - 2.0 * head(y[0], j)
        summed = summed + alpha * (got[mine, 1] - bend * column_own)
        for k in range(j):
            x = x - us[k][...] * head(ws[k][0], j) - ws[k][...] * head(us[k][0], j)
    x = jnp.where(ids > j, x, 0.0)
    norm = jnp.sqrt(dot(x, x))
    scale = 1.0 / jnp.sqrt(2.0 * norm * (norm + head(x[0], j + 1)) + EPS)
    u = (x + jnp.where(ids == j + 1, norm, 0.0)) * scale
    u_out[...] = u
    product_own = (summed + norm * next_own) * scale
    for k in range(j):
        for n, v in ((k, ws[k]), (K + k, us[k])):
            coeffs[n] = (dot(v[...], x) + norm * head(v[0], j + 1)) * scale
    if j == K - 1:
        send(payload, [product_own])
        return
    y_own = product_own
    x_own = next_own
    for k in range(j):
        u_own, w_own = us[k][mine], ws[k][mine]
        y_own = y_own - u_own * coeffs[k] - w_own * coeffs[K + k]
        x_own = x_own - u_own * head(ws[k][0], j + 1) - w_own * head(us[k][0], j + 1)
    x_own = x_own - 2.0 * head(u[0], j + 1) * y_own
    x_own = jnp.where(own_ids(mine) > j + 1, x_own, 0.0)
    x_ref[...] = x_own
    if j % 2:
        times_rows(tile, x_ref, product)
        send(payload, [product[...], product_own, spare[j - 1, 2], spare[j, 2]])
    else:
        times_cols(tile, x_own, product)
        send(payload, [product[...], product_own] + ([spare[0, 2]] if j == 0 else []))


def thirds(value):
    high = value.astype(jnp.bfloat16).astype(F32)
    rest = value - high
    middle = rest.astype(jnp.bfloat16).astype(F32)
    return high, middle, rest - middle


def last_kernel(place, got, coeffs, *refs):
    us, ws = refs[:K], refs[K : 2 * K - 1]
    tile, updated, images, right, result, sem = refs[2 * K - 1 :]
    gamma = rayleigh(K - 1, got[:, 0], us[K - 1][...], coeffs)
    shares = []
    for mine in (place[0], place[1]):
        u_own, w_own = [v[mine] for v in us], [v[mine] for v in ws]
        _, w = image(K - 1, got[mine, 0], u_own, w_own, coeffs, gamma)
        shares.append((u_own, [*w_own, w]))
    (u_row, w_row), (u_col, w_col) = shares
    for k in range(K):
        images[k] = w_row[k]
    pad = jnp.zeros((32, 128), F32)
    for b in range(8):
        high, middle, low = thirds(jnp.concatenate([v[b : b + 1] for v in [*w_col, *u_col]], axis=0))
        right[:, 128 * b : 128 * (b + 1)] = jnp.concatenate(
            [high, middle, high, low, middle, high, pad], axis=0
        ).astype(jnp.bfloat16)
    copies = []
    for a in range(8):
        high, middle, low = thirds(jnp.concatenate([v[a : a + 1] for v in [*u_row, *w_row]], axis=0))
        left = jnp.concatenate([high, high, middle, high, middle, low, pad], axis=0).T.astype(jnp.bfloat16)
        change = jnp.dot(left, right[...], preferred_element_type=F32)
        for b in range(8):
            block = tile[b, pl.ds(128 * a, 128), :] - change[:, 128 * b : 128 * (b + 1)]
            result[pl.ds(1024 * a + b, 128, stride=8), :] = block
        copies.append(
            pltpu.make_async_copy(
                result.at[pl.ds(1024 * a, 1024), :], updated.at[pl.ds(1024 * a, 1024), :], sem.at[a]
            )
        )
        copies[-1].start()
    for copy in copies:
        copy.wait()


def params(limit=SCOPED):
    return pltpu.CompilerParams(vmem_limit_bytes=limit)


def cost(flops, moved):
    return pl.CostEstimate(flops=flops, bytes_accessed=moved, transcendentals=0)


def exchange(payload, axis):
    return lax.all_to_all(payload, axis, split_axis=0, concat_axis=0, tiled=True)


def body(matrix):
    whole = jax.ShapeDtypeStruct((PEERS, 8, 128), F32)
    native = matrix.reshape(1024, 8, 128)
    place = jnp.stack([lax.axis_index("row"), lax.axis_index("col")]).astype(jnp.int32)
    hbm = pl.BlockSpec(memory_space=pltpu.HBM)
    payload = pl.pallas_call(
        panel_kernel,
        out_shape=jax.ShapeDtypeStruct((PEERS, 3, 8, 128), F32),
        in_specs=[hbm],
        out_specs=vmem(),
        scratch_shapes=[
            pltpu.VMEM((1024, 128), F32),
            pltpu.VMEM((K + 1, 8, 128), F32),
            pltpu.SemaphoreType.DMA((8,)),
        ],
        compiler_params=params(WIDE),
        cost_estimate=cost(2**20, 2**20),
    )(native)
    panel = exchange(payload, "col")
    streamed, plain = pl.pallas_call(
        load_kernel,
        out_shape=(
            jax.ShapeDtypeStruct((40, 1024, 128), F32),
            jax.ShapeDtypeStruct((8, 1024, 128), F32),
        ),
        in_specs=[hbm],
        out_specs=[hbm, hbm],
        scratch_shapes=[
            pltpu.VMEM((8, 1024, 128), F32),
            pltpu.SemaphoreType.DMA((8,)),
            pltpu.SemaphoreType.DMA((2, 8)),
        ],
        compiler_params=params(WIDE),
        cost_estimate=cost(2**21, 2**23),
    )(native)
    payload, tile = pl.pallas_call(
        first_kernel,
        out_shape=(
            jax.ShapeDtypeStruct((PEERS, 3, 8, 128), F32),
            jax.ShapeDtypeStruct((8, 1024, 128), F32),
        ),
        in_specs=[smem(), vmem(), hbm],
        out_specs=[vmem(), vmem()],
        scratch_shapes=[
            pltpu.VMEM((8, 128), F32),
            pltpu.VMEM((1024, 128), F32),
            pltpu.SemaphoreType.DMA((8,)),
        ],
        compiler_params=params(48000000),
        cost_estimate=cost(2**21, 2**22),
    )(place, panel, streamed)
    us, ws, coeffs, before = [], [], None, None
    for j in range(K):
        got = exchange(payload, "col" if j % 2 else "row")
        inputs = [place, got]
        if j == 0:
            inputs.append(panel)
        if j == 1:
            spare = got
        elif j % 2:
            inputs.append(spare)
        if j % 2:
            inputs.append(before)
        if j < K - 1:
            inputs.append(tile)
        inputs += us + ws
        if j > 0:
            inputs.append(coeffs)
        sent = 1 if j == K - 1 else 3 if j == 0 else 4 if j % 2 else 2
        outs = [jax.ShapeDtypeStruct((PEERS, sent, 8, 128), F32), whole, whole]
        if j > 0:
            outs.append(whole)
        results = pl.pallas_call(
            functools.partial(step_kernel, j),
            out_shape=outs,
            in_specs=[smem()] + [vmem()] * (len(inputs) - 1),
            out_specs=[vmem()] * len(outs),
            scratch_shapes=[pltpu.VMEM((8, 128), F32)] * 2,
            compiler_params=params(),
            cost_estimate=cost(2**21, 2**22),
            name=f"step_{j}",
        )(*inputs)
        payload, coeffs = results[0], results[2]
        us.append(results[1])
        if j > 0:
            ws.append(results[3])
        before = got
    got = exchange(payload, "row")
    updated, images = pl.pallas_call(
        last_kernel,
        out_shape=(jax.ShapeDtypeStruct((8192, 128), F32), jax.ShapeDtypeStruct((K, 8, 128), F32)),
        in_specs=[smem()] + [vmem()] * (2 * K + 2),
        out_specs=[hbm, vmem()],
        scratch_shapes=[
            pltpu.VMEM((128, 1024), jnp.bfloat16),
            pltpu.VMEM((8192, 128), F32),
            pltpu.SemaphoreType.DMA((8,)),
        ],
        compiler_params=params(),
        cost_estimate=cost(2**25, 2**23),
    )(place, got, coeffs, *us, *ws, plain)
    return updated.reshape(matrix.shape), images.reshape(K, 8, 1, 128)


def solution(mesh):
    spec = P(None, "row", None, None, "col", None)
    return jax.shard_map(
        body, mesh=mesh, in_specs=(spec,), out_specs=(spec, P(None, None, "row", None)), check_vma=False
    )
```

```python
import functools

import jax
import jax.numpy as jnp
from jax import lax
from jax.experimental import pallas as pl
from jax.experimental.pallas import tpu as pltpu
from jax.sharding import PartitionSpec as P

K = 8
EPS = 1e-06
PEERS = 16
F32 = jnp.float32
SCOPED = 16 * 1024 * 1024
WIDE = 62000000


def vmem():
    return pl.BlockSpec(memory_space=pltpu.VMEM)


def smem():
    return pl.BlockSpec(memory_space=pltpu.SMEM)


def head(slab, entry):
    return jnp.broadcast_to(slab[0:1, entry : entry + 1], slab.shape)


def total(slab):
    by_lane = jnp.sum(slab, axis=0, keepdims=True)
    return jnp.broadcast_to(jnp.sum(by_lane, axis=1, keepdims=True), slab.shape)


def dot(left, right):
    return total(jnp.sum(left * right, axis=0))


def slab_index(shape, axis):
    return lax.broadcasted_iota(jnp.int32, shape, axis)


def full_ids():
    shape = (PEERS, 8, 128)
    first = (slab_index(shape, 0) == 0) & (slab_index(shape, 1) == 0)
    return jnp.where(first, slab_index(shape, 2), 1024)


def own_ids(mine):
    shape = (8, 128)
    first = (slab_index(shape, 0) == 0) & (mine == 0)
    return jnp.where(first, slab_index(shape, 1), 1024)


def times_cols(tile, x, out):
    for a in range(8):
        rows = pl.ds(a * 128, 128)
        acc = tile[0, rows, :] * x[0:1, :]
        for b in range(1, 8):
            acc += tile[b, rows, :] * x[b : b + 1, :]
        out[a : a + 1, :] = jnp.sum(acc.T, axis=0, keepdims=True)


def times_rows(tile, x_ref, out):
    sums = [jnp.zeros((8, 128), F32)] * 8
    for a in range(8):
        x = jnp.broadcast_to(x_ref[a : a + 1, :], (128, 128)).T
        for b in range(8):
            line = tile[b, pl.ds(a * 128, 128), :] * x
            sums[b] += jnp.sum(line.reshape(16, 8, 128), axis=0)
    for b in range(8):
        out[b : b + 1, :] = jnp.sum(sums[b], axis=0, keepdims=True)


def send(payload, slabs):
    for n, slab in enumerate(slabs):
        for q in range(PEERS):
            payload[q, n] = slab


def panel_kernel(matrix, payload, corner, panel, sem):
    copy = pltpu.make_async_copy(matrix.at[:, 0, :], corner, sem)
    copy.start()
    copy.wait()
    for a in range(8):
        lines = corner[pl.ds(128 * a, 128), :].T
        for k in range(K + 1):
            panel[k, a : a + 1, :] = lines[k : k + 1, :]
    for q in range(PEERS):
        payload[q, 0] = panel[0]
        payload[q, 1] = panel[1]
        payload[q, 2] = panel[2 + q % (K - 1)]


def load_kernel(matrix, tile, spare, held, fetched, stored):
    into = [pltpu.make_async_copy(matrix.at[:, b, :], held.at[b], fetched.at[b]) for b in range(8)]
    out = [
        pltpu.make_async_copy(held.at[b], ref.at[b], stored.at[n, b])
        for b in range(8)
        for n, ref in enumerate((tile, spare))
    ]
    for copy in into:
        copy.start()
    for b in range(8):
        into[b].wait()
        out[2 * b].start()
        out[2 * b + 1].start()
    for copy in out:
        copy.wait()


def first_kernel(place, panel, tile, payload, held, x_ref, lines, sem):
    copies = [pltpu.make_async_copy(tile.at[b], held.at[b], sem.at[b]) for b in range(8)]
    for copy in copies:
        copy.start()
    x_ref[...] = jnp.where(own_ids(place[0]) > 0, panel[0, 0], 0.0)
    for a in range(8):
        lines[pl.ds(128 * a, 128), :] = jnp.broadcast_to(x_ref[a : a + 1, :], (128, 128)).T
    for b in range(8):
        copies[b].wait()
        line = jnp.sum((held[b] * lines[...]).reshape(128, 8, 128), axis=0)
        line = jnp.sum(line, axis=0, keepdims=True)
        for q in range(PEERS):
            payload[q, 0, b : b + 1, :] = line
    for q in range(PEERS):
        payload[q, 1] = panel[0, 0]
        payload[q, 2] = panel[0, 1]


def rayleigh(j, product, u, coeffs):
    gamma = dot(u, product)
    for k in range(j):
        gamma = gamma - 2.0 * coeffs[k] * coeffs[K + k]
    return gamma


def image(j, product, us, ws, coeffs, gamma):
    y = product
    for k in range(j):
        y = y - us[k] * coeffs[k] - ws[k] * coeffs[K + k]
    return y, 2.0 * y - 2.0 * gamma * us[j]


def step_kernel(j, *refs):
    refs = list(refs)
    place, got = refs[:2]
    del refs[:2]
    spare = got if j == 1 else refs.pop(0) if j == 0 or j % 2 else None
    late = refs.pop(0) if j % 2 else got
    tile = refs.pop(0) if j < K - 1 else None
    us = [refs.pop(0) for _ in range(j)]
    ws = [refs.pop(0) for _ in range(max(j - 1, 0))]
    coeffs_before = refs.pop(0) if j > 0 else None
    payload, u_out, coeffs = refs[:3]
    del refs[:3]
    if j > 0:
        w_out = refs.pop(0)
    x_ref, product = refs
    mine = place[(j + 1) % 2]
    ids = full_ids()
    summed = got[0, 0]
    for q in range(1, PEERS):
        summed = summed + got[q, 0]
    at = {0: 1, 1: 2}.get(j, 3 if j % 2 else 2)
    column, column_own = late[:, at], late[mine, at]
    next_own = spare[j - 1, 2] if j % 2 else late[mine, at + 1]
    x = column
    if j > 0:
        before = got[:, 1]
        gamma = rayleigh(j - 1, before, us[j - 1][...], coeffs_before)
        y, w = image(
            j - 1, before, [v[...] for v in us], [v[...] for v in ws], coeffs_before, gamma
        )
        w_out[...] = w
        ws = ws + [w_out]
        bend = head(us[j - 1][0], j)
        alpha = 4.0 * gamma * bend - 2.0 * head(y[0], j)
        summed = summed + alpha * (got[mine, 1] - bend * column_own)
        for k in range(j):
            x = x - us[k][...] * head(ws[k][0], j) - ws[k][...] * head(us[k][0], j)
    x = jnp.where(ids > j, x, 0.0)
    norm = jnp.sqrt(dot(x, x))
    scale = 1.0 / jnp.sqrt(2.0 * norm * (norm + head(x[0], j + 1)) + EPS)
    u = (x + jnp.where(ids == j + 1, norm, 0.0)) * scale
    u_out[...] = u
    product_own = (summed + norm * next_own) * scale
    for k in range(j):
        for n, v in ((k, ws[k]), (K + k, us[k])):
            coeffs[n] = (dot(v[...], x) + norm * head(v[0], j + 1)) * scale
    if j == K - 1:
        send(payload, [product_own])
        return
    y_own = product_own
    x_own = next_own
    for k in range(j):
        u_own, w_own = us[k][mine], ws[k][mine]
        y_own = y_own - u_own * coeffs[k] - w_own * coeffs[K + k]
        x_own = x_own - u_own * head(ws[k][0], j + 1) - w_own * head(us[k][0], j + 1)
    x_own = x_own - 2.0 * head(u[0], j + 1) * y_own
    x_own = jnp.where(own_ids(mine) > j + 1, x_own, 0.0)
    x_ref[...] = x_own
    if j % 2:
        times_rows(tile, x_ref, product)
        send(payload, [product[...], product_own, spare[j - 1, 2], spare[j, 2]])
    else:
        times_cols(tile, x_own, product)
        send(payload, [product[...], product_own] + ([spare[0, 2]] if j == 0 else []))


def thirds(value):
    high = value.astype(jnp.bfloat16).astype(F32)
    rest = value - high
    middle = rest.astype(jnp.bfloat16).astype(F32)
    return high, middle, rest - middle


def last_kernel(place, got, coeffs, *refs):
    us, ws = refs[:K], refs[K : 2 * K - 1]
    tile, updated, images, right, result, sem = refs[2 * K - 1 :]
    gamma = rayleigh(K - 1, got[:, 0], us[K - 1][...], coeffs)
    shares = []
    for mine in (place[0], place[1]):
        u_own, w_own = [v[mine] for v in us], [v[mine] for v in ws]
        _, w = image(K - 1, got[mine, 0], u_own, w_own, coeffs, gamma)
        shares.append((u_own, [*w_own, w]))
    (u_row, w_row), (u_col, w_col) = shares
    for k in range(K):
        images[k] = w_row[k]
    pad = jnp.zeros((32, 128), F32)
    for b in range(8):
        high, middle, low = thirds(jnp.concatenate([v[b : b + 1] for v in [*w_col, *u_col]], axis=0))
        right[:, 128 * b : 128 * (b + 1)] = jnp.concatenate(
            [high, middle, high, low, middle, high, pad], axis=0
        ).astype(jnp.bfloat16)
    copies = []
    for a in range(8):
        high, middle, low = thirds(jnp.concatenate([v[a : a + 1] for v in [*u_row, *w_row]], axis=0))
        left = jnp.concatenate([high, high, middle, high, middle, low, pad], axis=0).T.astype(jnp.bfloat16)
        change = jnp.dot(left, right[...], preferred_element_type=F32)
        for b in range(8):
            block = tile[b, pl.ds(128 * a, 128), :] - change[:, 128 * b : 128 * (b + 1)]
            result[pl.ds(1024 * a + b, 128, stride=8), :] = block
        copies.append(
            pltpu.make_async_copy(
                result.at[pl.ds(1024 * a, 1024), :], updated.at[pl.ds(1024 * a, 1024), :], sem.at[a]
            )
        )
        copies[-1].start()
    for copy in copies:
        copy.wait()


def params(limit=SCOPED):
    return pltpu.CompilerParams(vmem_limit_bytes=limit)


def cost(flops, moved):
    return pl.CostEstimate(flops=flops, bytes_accessed=moved, transcendentals=0)


def exchange(payload, axis):
    return lax.all_to_all(payload, axis, split_axis=0, concat_axis=0, tiled=True)


def body(matrix):
    whole = jax.ShapeDtypeStruct((PEERS, 8, 128), F32)
    native = matrix.reshape(1024, 8, 128)
    place = jnp.stack([lax.axis_index("row"), lax.axis_index("col")]).astype(jnp.int32)
    hbm = pl.BlockSpec(memory_space=pltpu.HBM)
    payload = pl.pallas_call(
        panel_kernel,
        out_shape=jax.ShapeDtypeStruct((PEERS, 3, 8, 128), F32),
        in_specs=[hbm],
        out_specs=vmem(),
        scratch_shapes=[
            pltpu.VMEM((1024, 128), F32),
            pltpu.VMEM((K + 1, 8, 128), F32),
            pltpu.SemaphoreType.DMA,
        ],
        compiler_params=params(WIDE),
        cost_estimate=cost(2**20, 2**20),
    )(native)
    panel = exchange(payload, "col")
    streamed, plain = pl.pallas_call(
        load_kernel,
        out_shape=(
            jax.ShapeDtypeStruct((40, 1024, 128), F32),
            jax.ShapeDtypeStruct((8, 1024, 128), F32),
        ),
        in_specs=[hbm],
        out_specs=[hbm, hbm],
        scratch_shapes=[
            pltpu.VMEM((8, 1024, 128), F32),
            pltpu.SemaphoreType.DMA((8,)),
            pltpu.SemaphoreType.DMA((2, 8)),
        ],
        compiler_params=params(WIDE),
        cost_estimate=cost(2**21, 2**23),
    )(native)
    payload, tile = pl.pallas_call(
        first_kernel,
        out_shape=(
            jax.ShapeDtypeStruct((PEERS, 3, 8, 128), F32),
            jax.ShapeDtypeStruct((8, 1024, 128), F32),
        ),
        in_specs=[smem(), vmem(), hbm],
        out_specs=[vmem(), vmem()],
        scratch_shapes=[
            pltpu.VMEM((8, 128), F32),
            pltpu.VMEM((1024, 128), F32),
            pltpu.SemaphoreType.DMA((8,)),
        ],
        compiler_params=params(48000000),
        cost_estimate=cost(2**21, 2**22),
    )(place, panel, streamed)
    us, ws, coeffs, before = [], [], None, None
    for j in range(K):
        got = exchange(payload, "col" if j % 2 else "row")
        inputs = [place, got]
        if j == 0:
            inputs.append(panel)
        if j == 1:
            spare = got
        elif j % 2:
            inputs.append(spare)
        if j % 2:
            inputs.append(before)
        if j < K - 1:
            inputs.append(tile)
        inputs += us + ws
        if j > 0:
            inputs.append(coeffs)
        sent = 1 if j == K - 1 else 3 if j == 0 else 4 if j % 2 else 2
        outs = [jax.ShapeDtypeStruct((PEERS, sent, 8, 128), F32), whole, whole]
        if j > 0:
            outs.append(whole)
        results = pl.pallas_call(
            functools.partial(step_kernel, j),
            out_shape=outs,
            in_specs=[smem()] + [vmem()] * (len(inputs) - 1),
            out_specs=[vmem()] * len(outs),
            scratch_shapes=[pltpu.VMEM((8, 128), F32)] * 2,
            compiler_params=params(),
            cost_estimate=cost(2**21, 2**22),
            name=f"step_{j}",
        )(*inputs)
        payload, coeffs = results[0], results[2]
        us.append(results[1])
        if j > 0:
            ws.append(results[3])
        before = got
    got = exchange(payload, "row")
    updated, images = pl.pallas_call(
        last_kernel,
        out_shape=(jax.ShapeDtypeStruct((8192, 128), F32), jax.ShapeDtypeStruct((K, 8, 128), F32)),
        in_specs=[smem()] + [vmem()] * (2 * K + 2),
        out_specs=[hbm, vmem()],
        scratch_shapes=[
            pltpu.VMEM((128, 1024), jnp.bfloat16),
            pltpu.VMEM((8192, 128), F32),
            pltpu.SemaphoreType.DMA((8,)),
        ],
        compiler_params=params(),
        cost_estimate=cost(2**25, 2**23),
    )(place, got, coeffs, *us, *ws, plain)
    return updated.reshape(matrix.shape), images.reshape(K, 8, 1, 128)


def solution(mesh):
    spec = P(None, "row", None, None, "col", None)
    return jax.shard_map(
        body, mesh=mesh, in_specs=(spec,), out_specs=(spec, P(None, None, "row", None)), check_vma=False
    )
```
